128 devices in a mesh: gz: 8 (over z, y_lo), gy: 16 (over x, y_hi, core).
Axes of the slice: x: 4, y: 4 (y_hi: 2, y_lo: 2; y = y_hi * 2 + y_lo), z: 4, core: 2. Of those that a mesh axis runs over, the one named last changes fastest.
Arguments:
- thermal_departure: float32 [8, 2048, 2048], P(None, 'gy', 'gz'), may hold values from -6 to 6
- speed_along_primary: float32 [8, 2048, 2048], P(None, 'gy', 'gz'), may hold values from -4 to 4
- speed_along_lateral: float32 [8, 2048, 2048], P(None, 'gy', 'gz'), may hold values from -4 to 4
- upward_speed: float32 [8, 2048, 2048], P(None, 'gy', 'gz'), may hold values from -4 to 4
- container_solid_markers: int32 [8, 2048, 2048], P(None, 'gy', 'gz'), may hold values 0 or 1
Outputs:
- temp_next: float32 [8, 2048, 2048], P(None, 'gy', 'gz')
- u_next: float32 [8, 2048, 2048], P(None, 'gy', 'gz')
- v_next: float32 [8, 2048, 2048], P(None, 'gy', 'gz')
- w_next: float32 [8, 2048, 2048], P(None, 'gy', 'gz')
- path_map: float32 [8, 2048], P('gz', 'gy')
The draws below stay inside these ranges and needn't reach their ends.
Inputs may be any that keep to these rules, and one draw needn't show every extreme that they name: `container_solid_markers`: 1 marks air, 0 a solid cell.
All inputs are finite; a program needn't handle non-finite values. No bound on the sum of `container_solid_markers` on one device may be relied on, other than what follows from the above.
Results may differ from the reference program's by a relative error of at most 0.00002.
Values sent between devices are 32-bit elements; how exact they have to be, the bound alone decides.
A program may use at most 128 MiB of HBM per device.

```python
import math
import jax
import jax.numpy as jnp
from jax import lax

SHEET_ROW_COUNT = 8
CY = 128
LATERAL_COUNT = 2048
ALTITUDE_COUNT = 2048
N_GY = 16


def with_ends(entries, own_key, low, high):
    extent = entries.shape
    place = [jax.random.randint(jax.random.fold_in(own_key, axis), (), 0, extent[axis]) for axis in range(len(extent))]
    entries = entries.at[tuple(place)].set(low)
    longest = extent.index(max(extent))
    place[longest] = (place[longest] + 1) % extent[longest]
    return entries.at[tuple(place)].set(high)


def shard_levels(key, dims, shards, smallest, top_value):
    factor_of, own = 1.0, jax.random.fold_in(key, 6)
    for dim, parts in shards:
        draws = jnp.exp(jax.random.uniform(jax.random.fold_in(own, dim), (parts,), jnp.float32, smallest / len(shards), top_value / len(shards)))
        factor_of = factor_of * jnp.repeat(draws, dims[dim] // parts).reshape([-1 if axis == dim else 1 for axis in range(len(dims))])
    return factor_of


def gaussian(stream_key, dims, spread, bound, split=(), held_as=jnp.bfloat16):
    result = jax.random.normal(stream_key, dims, jnp.float32) * spread
    if len(split) > 0:
        result = shard_levels(stream_key, dims, split, -0.22, 0.18) * result
    return jnp.clip(result, min=-bound, max=bound).astype(held_as)


def setup_inputs(seed: int = 0) -> dict:
    key_of = jax.random.split(jax.random.key(seed), 6)
    thermal_departure = gaussian(key_of[0], (SHEET_ROW_COUNT, LATERAL_COUNT, ALTITUDE_COUNT), 1.0, 6.0, ((1, 16), (2, 8)), jnp.float32)
    speed_along_primary = gaussian(key_of[1], (SHEET_ROW_COUNT, LATERAL_COUNT, ALTITUDE_COUNT), 1.0, 4.0, ((1, 16), (2, 8)), jnp.float32)
    speed_along_lateral = gaussian(key_of[2], (SHEET_ROW_COUNT, LATERAL_COUNT, ALTITUDE_COUNT), 1.0, 4.0, ((1, 16), (2, 8)), jnp.float32)
    upward_speed = gaussian(key_of[3], (SHEET_ROW_COUNT, LATERAL_COUNT, ALTITUDE_COUNT), 1.0, 4.0, ((1, 16), (2, 8)), jnp.float32)
    container_solid_markers = with_ends((jax.random.randint(key_of[4], (SHEET_ROW_COUNT, LATERAL_COUNT, ALTITUDE_COUNT), 0, 8) < 7).astype(jnp.int32), jax.random.fold_in(key_of[4], 1), 0, 1)
    return dict(thermal_departure=thermal_departure, speed_along_primary=speed_along_primary, speed_along_lateral=speed_along_lateral, upward_speed=upward_speed, container_solid_markers=container_solid_markers)


TIME_STEP = 0.1
NU_BASE = 0.05
KAPPA_BASE = 0.05
SMAG_COEF = 0.03
PRANDTL = 0.4
BUOYANCY = 0.5

def tendencies(padded):
    centre = padded[:, :, 1:-1, 1:-1]
    east_side = jnp.roll(centre, -1, 1)
    west_side = jnp.roll(centre, 1, 1)
    north_side = padded[:, :, 2:, 1:-1]
    south_side = padded[:, :, :-2, 1:-1]
    upper_side = padded[:, :, 1:-1, 2:]
    lower_side = padded[:, :, 1:-1, :-2]
    grad_x = 0.5 * (east_side - west_side)
    grad_y = 0.5 * (north_side - south_side)
    grad_z = 0.5 * (upper_side - lower_side)
    laplace = east_side + west_side + north_side + south_side + upper_side + lower_side - 6.0 * centre
    advect = centre[1] * grad_x + centre[2] * grad_y + centre[3] * grad_z
    strain = grad_x[1] * grad_x[1] + grad_y[2] * grad_y[2] + grad_z[3] * grad_z[3]
    shear_a = grad_y[1] + grad_x[2]
    shear_b = grad_z[1] + grad_x[3]
    shear_c = grad_z[2] + grad_y[3]
    strain = strain + 0.5 * (shear_a * shear_a + shear_b * shear_b + shear_c * shear_c)
    eddy_visc = SMAG_COEF * jnp.sqrt(2.0 * strain + 0.01)
    diffusion = jnp.stack([KAPPA_BASE + eddy_visc / PRANDTL, NU_BASE + eddy_visc, NU_BASE + eddy_visc, NU_BASE + eddy_visc])
    tendency = diffusion * laplace - advect
    buoyant = tendency[3] + BUOYANCY * centre[0]
    return jnp.stack([tendency[0], tendency[1], tendency[2], buoyant])

def masked(fluid_unknowns, fluid_mask):
    return jnp.concatenate([fluid_unknowns[:1], fluid_unknowns[1:] * fluid_mask[None]], 0)

def full_rates(fluid_unknowns):
    wrapped = jnp.concatenate([fluid_unknowns[:, :, -1:], fluid_unknowns, fluid_unknowns[:, :, :1]], 2)
    padded = jnp.pad(wrapped, ((0, 0), (0, 0), (0, 0), (1, 1)))

    def by_block(block_index):
        piece = lax.dynamic_slice_in_dim(padded, block_index * CY, CY + 2, 2)
        return tendencies(piece)
    pieces = lax.map(by_block, jnp.arange(N_GY, dtype=jnp.int32))
    return jnp.moveaxis(pieces, 0, 2).reshape(4, SHEET_ROW_COUNT, LATERAL_COUNT, ALTITUDE_COUNT)

def reference(thermal_departure, speed_along_primary, speed_along_lateral, upward_speed, container_solid_markers):
    fluid_mask = container_solid_markers.astype(jnp.float32)
    fluid_unknowns = jnp.stack([thermal_departure, speed_along_primary, speed_along_lateral, upward_speed])
    section_one = masked(fluid_unknowns + TIME_STEP * full_rates(fluid_unknowns), fluid_mask)
    section_two = masked(0.5 * fluid_unknowns + 0.5 * (section_one + TIME_STEP * full_rates(section_one)), fluid_mask)
    refraction = 8.0 * (1.0 - jnp.exp(-section_two[0] / 8.0))
    path_map = lax.optimization_barrier(jnp.sum(refraction, axis=2)) / math.sqrt(ALTITUDE_COUNT)
    return (section_two[0], section_two[1], section_two[2], section_two[3], path_map)
```

```python
import math

import jax
import jax.numpy as jnp
from jax import lax
from jax.experimental import pallas as pl
from jax.experimental.pallas import tpu as pltpu
from jax.sharding import PartitionSpec as P

MESH = pl.DeviceIdType.MESH
NX, NY, LANES = 8, 128, 128
NGZ, NGY = 8, 16
UNROLL = 2
F32 = jnp.float32


def lane_index():
    return lax.broadcasted_iota(jnp.int32, (NX, LANES), 1)


def advance(c, e, w, n, s, u, l):
    dx = [e[i] - w[i] for i in range(4)]
    dy = [n[i] - s[i] for i in range(4)]
    dz = [u[i] - l[i] for i in range(4)]
    shear_a = dy[1] + dx[2]
    shear_b = dz[1] + dx[3]
    shear_c = dz[2] + dy[3]
    normal = dx[1] * dx[1] + dy[2] * dy[2] + dz[3] * dz[3]
    shear = shear_a * shear_a + shear_b * shear_b + shear_c * shear_c
    arg = 4.5e-6 * normal + 2.25e-6 * shear + 9e-8
    eddy = arg * lax.rsqrt(arg)
    k_vel = eddy + 0.005
    k_heat = 2.5 * eddy + 0.005
    rest_vel = 1.0 - 6.0 * k_vel
    rest_heat = 1.0 - 6.0 * k_heat
    au = -0.05 * c[1]
    av = -0.05 * c[2]
    aw = -0.05 * c[3]
    out = []
    for i in range(4):
        around = (e[i] + w[i]) + (n[i] + s[i]) + (u[i] + l[i])
        k, rest = (k_heat, rest_heat) if i == 0 else (k_vel, rest_vel)
        out.append(k * around + rest * c[i] + (au * dx[i] + av * dy[i] + aw * dz[i]))
    out[3] = out[3] + 0.05 * c[0]
    return out


def around_x(v):
    return pltpu.roll(v, NX - 1, 0), pltpu.roll(v, 1, 0)


def kernel(
    t_hbm, u_hbm, v_hbm, w_hbm, m_hbm,
    t_out, u_out, v_out, w_out, path_out,
    s0, s1, mk, own, got, corner, got_corner, ring, part, got_part, res,
    in_sem, out_sem, ysend, yrecv, zsend, zrecv, csend, crecv, psend, precv,
):
    gz = lax.axis_index("gz")
    gy = lax.axis_index("gy")
    zup, zdn = lax.rem(gz + 1, NGZ), lax.rem(gz + NGZ - 1, NGZ)
    yup, ydn = lax.rem(gy + 1, NGY), lax.rem(gy + NGY - 1, NGY)
    lane = lane_index()
    first, last = lane == 0, lane == LANES - 1

    barrier = pltpu.get_barrier_semaphore()
    partners = [(gz, yup), (gz, ydn), (zup, yup), (zup, ydn), (zdn, yup), (zdn, ydn)]
    partners += [(lax.rem(gz + d, NGZ), gy) for d in range(1, NGZ)]
    for a, b in partners:
        pl.semaphore_signal(barrier, inc=1, device_id=(a, b), device_id_type=MESH)

    srcs = (t_hbm, u_hbm, v_hbm, w_hbm)
    for f in range(4):
        for h in range(2):
            for x in range(NX):
                pltpu.make_async_copy(
                    srcs[f].at[x, :, pl.ds(h * LANES, LANES)],
                    s0.at[f, h, pl.ds(2, NY), x, :],
                    in_sem.at[f],
                ).start()
    for h in range(2):
        for x in range(NX):
            pltpu.make_async_copy(
                m_hbm.at[x, :, pl.ds(h * LANES, LANES)],
                mk.at[h, pl.ds(1, NY), x, :],
                in_sem.at[4],
            ).start()

    zero = jnp.zeros((NX, LANES), F32)

    def pack(load):
        def body(y, carry):
            l0, l1, r0, r1 = carry
            a, b = load(0, y), load(1, y)
            ra = pltpu.roll(a, y, 1)
            rb = pltpu.roll(b, y + 1, 1)
            here = lane == y
            l0 = jnp.where(here, ra, l0)
            l1 = jnp.where(lane == lax.rem(y + 1, LANES), ra, l1)
            r1 = jnp.where(here, rb, r1)
            r0 = jnp.where(lane == lax.rem(y + LANES - 1, LANES), rb, r0)
            return l0, l1, r0, r1

        l0, l1, r0, r1 = lax.fori_loop(0, NY, body, (zero,) * 4, unroll=8)
        return l0, pltpu.roll(l1, LANES - 1, 1), pltpu.roll(r0, 1, 1), r1

    corner_l, corner_r = zero, zero
    for f in range(4):
        whole = s0.at[f, :, pl.ds(2, NY), :, :]
        pltpu.make_async_copy(whole, whole, in_sem.at[f]).wait()
        l0, l1, r0, r1 = pack(lambda h, y, f=f: s0[f, h, y + 2])
        own[0, f, 0] = l0
        own[0, f, 1] = l1
        own[1, f, 0] = r0
        own[1, f, 1] = r1
        corner_l = jnp.where(lane == f, pltpu.roll(l0, f, 1), corner_l)
        corner_l = jnp.where(lane == 124 + f, pltpu.roll(l0, (f + 125) % LANES, 1), corner_l)
        corner_r = jnp.where(lane == f, pltpu.roll(r1, f, 1), corner_r)
        corner_r = jnp.where(lane == 124 + f, pltpu.roll(r1, (f + 125) % LANES, 1), corner_r)
    whole = mk.at[:, pl.ds(1, NY), :, :]
    pltpu.make_async_copy(whole, whole, in_sem.at[4]).wait()
    l0, _, _, r1 = pack(lambda h, y: mk[h, y + 1].astype(F32))
    own[0, 4, 0] = l0
    own[1, 4, 1] = r1
    own[0, 4, 1] = zero
    own[1, 4, 0] = zero
    corner[0] = corner_l
    corner[1] = corner_r

    pl.semaphore_wait(barrier, len(partners))

    def remote(src, dst, ssem, rsem, dev):
        return pltpu.make_async_remote_copy(
            src_ref=src, dst_ref=dst, send_sem=ssem, recv_sem=rsem,
            device_id=dev, device_id_type=MESH,
        )

    z_copies = [
        remote(own.at[0], got.at[1], zsend.at[0], zrecv.at[0], (zdn, gy)),
        remote(own.at[1], got.at[0], zsend.at[1], zrecv.at[1], (zup, gy)),
    ]
    c_copies = [
        remote(corner.at[0], got_corner.at[1, 1], csend.at[0], crecv.at[0], (zdn, ydn)),
        remote(corner.at[0], got_corner.at[1, 0], csend.at[1], crecv.at[1], (zdn, yup)),
        remote(corner.at[1], got_corner.at[0, 1], csend.at[2], crecv.at[2], (zup, ydn)),
        remote(corner.at[1], got_corner.at[0, 0], csend.at[3], crecv.at[3], (zup, yup)),
    ]
    y_copies = [
        remote(s0.at[:, :, pl.ds(2, 2)], s0.at[:, :, pl.ds(NY + 2, 2)], ysend.at[0], yrecv.at[0], (gz, ydn)),
        remote(s0.at[:, :, pl.ds(NY, 2)], s0.at[:, :, pl.ds(0, 2)], ysend.at[1], yrecv.at[1], (gz, yup)),
        remote(mk.at[:, 1], mk.at[:, NY + 1], ysend.at[2], yrecv.at[2], (gz, ydn)),
        remote(mk.at[:, NY], mk.at[:, 0], ysend.at[3], yrecv.at[3], (gz, yup)),
    ]
    for cp in z_copies + c_copies + y_copies:
        cp.start()
    for cp in z_copies:
        cp.wait()

    bottom, top = gz == 0, gz == NGZ - 1
    for f in range(4):
        for i in range(2):
            got[0, f, i] = jnp.where(bottom, 0.0, got[0, f, i])
            got[1, f, i] = jnp.where(top, 0.0, got[1, f, i])

    def rows(src, j, below, above):
        halves = []
        ca = [src[f, 0, j] for f in range(4)]
        cb = [src[f, 1, j] for f in range(4)]
        ap = [pltpu.roll(v, 1, 1) for v in ca]
        bp = [pltpu.roll(v, 1, 1) for v in cb]
        am = [pltpu.roll(v, LANES - 1, 1) for v in ca]
        bm = [pltpu.roll(v, LANES - 1, 1) for v in cb]
        for h, c in ((0, ca), (1, cb)):
            if h == 0:
                lo = [jnp.where(first, below[f], ap[f]) for f in range(4)]
                up = [jnp.where(last, bm[f], am[f]) for f in range(4)]
            else:
                lo = [jnp.where(first, ap[f], bp[f]) for f in range(4)]
                up = [jnp.where(last, above[f], bm[f]) for f in range(4)]
            ew = [around_x(v) for v in c]
            n = [src[f, h, j + 1] for f in range(4)]
            s = [src[f, h, j - 1] for f in range(4)]
            halves.append(advance(c, [p[0] for p in ew], [p[1] for p in ew], n, s, up, lo))
        return ca, cb, halves

    def row_one(y, ends):
        below, above = ends
        halves = rows(s0, y + 2, below, above)[2]
        for h in range(2):
            m = mk[h, y + 1].astype(F32)
            s1[0, h, y + 1] = halves[h][0]
            for f in range(1, 4):
                s1[f, h, y + 1] = halves[h][f] * m

    def loop_one(y, carry):
        to_first = lax.rem(LANES - y, LANES)
        below = [pltpu.roll(got[0, f, 1], to_first, 1) for f in range(4)]
        above = [pltpu.roll(got[1, f, 0], LANES - 1 - y, 1) for f in range(4)]
        row_one(y, (below, above))
        return carry

    lax.fori_loop(1, NY - 1, loop_one, 0, unroll=UNROLL)

    for cp in c_copies + y_copies:
        cp.wait()
    loop_one(0, 0)
    loop_one(NY - 1, 0)

    ends = []
    for side in range(2):
        for f in range(4):
            lo = pltpu.roll(got_corner[side, 0], (3 - f) % LANES, 1)
            hi = pltpu.roll(got_corner[side, 1], (LANES - f) % LANES, 1)
            v = jnp.where(last, lo, hi)
            ends.append(jnp.where(bottom if side == 0 else top, 0.0, v))
    end_of = lambda side, f: ends[side * 4 + f]

    row_one(-1, (
        [pltpu.roll(end_of(0, f), 1, 1) for f in range(4)],
        [end_of(1, f) for f in range(4)],
    ))
    row_one(NY, (
        [end_of(0, f) for f in range(4)],
        [pltpu.roll(end_of(1, f), LANES - 1, 1) for f in range(4)],
    ))
    for side in range(2):
        if side == 0:
            c = [got[0, f, 1] for f in range(4)]
            lo = [got[0, f, 0] for f in range(4)]
            up = [own[0, f, 0] for f in range(4)]
            m = got[0, 4, 1]
        else:
            c = [got[1, f, 0] for f in range(4)]
            lo = [own[1, f, 1] for f in range(4)]
            up = [got[1, f, 1] for f in range(4)]
            m = got[1, 4, 0]
        n = [jnp.where(last, pltpu.roll(end_of(side, f), LANES - 1, 1), pltpu.roll(c[f], LANES - 1, 1)) for f in range(4)]
        s = [jnp.where(first, pltpu.roll(end_of(side, f), 1, 1), pltpu.roll(c[f], 1, 1)) for f in range(4)]
        ew = [around_x(v) for v in c]
        new = advance(c, [p[0] for p in ew], [p[1] for p in ew], n, s, up, lo)
        outside = bottom if side == 0 else top
        for f in range(4):
            v = new[f] if f == 0 else new[f] * m
            ring[side, f] = jnp.where(outside, 0.0, v)

    outs = (t_out, u_out, v_out, w_out)

    def loop_two(y, acc):
        to_first = lax.rem(LANES - y, LANES)
        below = [pltpu.roll(ring[0, f], to_first, 1) for f in range(4)]
        above = [pltpu.roll(ring[1, f], LANES - 1 - y, 1) for f in range(4)]
        halves = rows(s1, y + 1, below, above)[2]
        total = None
        for h in range(2):
            m = 0.5 * mk[h, y + 1].astype(F32)
            for f in range(4):
                v = s0[f, h, y + 2] + halves[h][f]
                v = 0.5 * v if f == 0 else v * m
                res[f, h, y] = v
                if f == 0:
                    r = 1.0 - jnp.exp(-0.125 * v)
                    total = r if total is None else total + r
        return jnp.where(lane == y, jnp.sum(total, axis=1, keepdims=True), acc)

    acc = lax.fori_loop(0, NY, loop_two, zero, unroll=UNROLL)

    for f in range(4):
        for h in range(2):
            for x in range(NX):
                pltpu.make_async_copy(
                    res.at[f, h, :, x, :],
                    outs[f].at[x, :, pl.ds(h * LANES, LANES)],
                    out_sem.at[f],
                ).start()

    part[...] = acc
    copies = []
    for d in range(1, NGZ):
        peer = lax.rem(gz + d, NGZ)
        copies.append(remote(
            part.at[pl.ds(peer, 1)], got_part.at[d - 1], psend.at[d - 1], precv.at[d - 1], (peer, gy),
        ))
    for cp in copies:
        cp.start()
    total = part[pl.ds(gz, 1)]
    for cp in copies:
        cp.wait()
    for d in range(NGZ - 1):
        total = total + got_part[d]
    path_out[...] = total * (8.0 / math.sqrt(2048.0))

    for f in range(4):
        whole = res.at[f]
        pltpu.make_async_copy(whole, whole, out_sem.at[f]).wait()


def on_device(*args):
    block = jax.ShapeDtypeStruct((NX, NY, 2 * LANES), F32)
    anywhere = pl.BlockSpec(memory_space=pl.ANY)
    return pl.pallas_call(
        kernel,
        out_shape=(block, block, block, block, jax.ShapeDtypeStruct((1, NY), F32)),
        in_specs=[anywhere] * 5,
        out_specs=(anywhere,) * 4 + (pl.BlockSpec(memory_space=pltpu.VMEM),),
        scratch_shapes=[
            pltpu.VMEM((4, 2, NY + 4, NX, LANES), F32),
            pltpu.VMEM((4, 2, NY + 2, NX, LANES), F32),
            pltpu.VMEM((2, NY + 2, NX, LANES), jnp.int32),
            pltpu.VMEM((2, 5, 2, NX, LANES), F32),
            pltpu.VMEM((2, 5, 2, NX, LANES), F32),
            pltpu.VMEM((2, NX, LANES), F32),
            pltpu.VMEM((2, 2, NX, LANES), F32),
            pltpu.VMEM((2, 4, NX, LANES), F32),
            pltpu.VMEM((NX, LANES), F32),
            pltpu.VMEM((NGZ - 1, 1, LANES), F32),
            pltpu.VMEM((4, 2, NY, NX, LANES), F32),
            pltpu.SemaphoreType.DMA((5,)),
            pltpu.SemaphoreType.DMA((4,)),
            pltpu.SemaphoreType.DMA((4,)),
            pltpu.SemaphoreType.DMA((4,)),
            pltpu.SemaphoreType.DMA((2,)),
            pltpu.SemaphoreType.DMA((2,)),
            pltpu.SemaphoreType.DMA((4,)),
            pltpu.SemaphoreType.DMA((4,)),
            pltpu.SemaphoreType.DMA((NGZ - 1,)),
            pltpu.SemaphoreType.DMA((NGZ - 1,)),
        ],
        compiler_params=pltpu.CompilerParams(collective_id=0, has_side_effects=True),
        name="flow",
    )(*args)


def solution(mesh):
    split = P(None, "gy", "gz")
    return jax.shard_map(
        on_device,
        mesh=mesh,
        in_specs=(split,) * 5,
        out_specs=(split,) * 4 + (P("gz", "gy"),),
        check_vma=False,
    )
```

```python
import math

import jax
import jax.numpy as jnp
from jax import lax
from jax.experimental import pallas as pl
from jax.experimental.pallas import tpu as pltpu
from jax.sharding import PartitionSpec as P

MESH = pl.DeviceIdType.MESH
NX, NY, LANES = 8, 128, 128
NGZ, NGY = 8, 16
UNROLL = 2
F32 = jnp.float32


def lane_index():
    return lax.broadcasted_iota(jnp.int32, (NX, LANES), 1)


def advance(c, e, w, n, s, u, l):
    dx = [e[i] - w[i] for i in range(4)]
    dy = [n[i] - s[i] for i in range(4)]
    dz = [u[i] - l[i] for i in range(4)]
    shear_a = dy[1] + dx[2]
    shear_b = dz[1] + dx[3]
    shear_c = dz[2] + dy[3]
    normal = dx[1] * dx[1] + dy[2] * dy[2] + dz[3] * dz[3]
    shear = shear_a * shear_a + shear_b * shear_b + shear_c * shear_c
    arg = 4.5e-6 * normal + 2.25e-6 * shear + 9e-8
    eddy = arg * lax.rsqrt(arg)
    k_vel = eddy + 0.005
    k_heat = 2.5 * eddy + 0.005
    rest_vel = 1.0 - 6.0 * k_vel
    rest_heat = 1.0 - 6.0 * k_heat
    au = -0.05 * c[1]
    av = -0.05 * c[2]
    aw = -0.05 * c[3]
    out = []
    for i in range(4):
        around = (e[i] + w[i]) + (n[i] + s[i]) + (u[i] + l[i])
        k, rest = (k_heat, rest_heat) if i == 0 else (k_vel, rest_vel)
        out.append(k * around + rest * c[i] + (au * dx[i] + av * dy[i] + aw * dz[i]))
    out[3] = out[3] + 0.05 * c[0]
    return out


def around_x(v):
    return pltpu.roll(v, NX - 1, 0), pltpu.roll(v, 1, 0)


def kernel(
    t_hbm, u_hbm, v_hbm, w_hbm, m_hbm,
    res, path,
    s0, s1, mk, own, zsrc, got, merged, edges, corner, got_corner, ring, part, got_part,
    in_sem, ysend, yrecv, zsend, zrecv, csend, crecv, psend, precv,
):
    gz = lax.axis_index("gz")
    gy = lax.axis_index("gy")
    zup, zdn = lax.rem(gz + 1, NGZ), lax.rem(gz + NGZ - 1, NGZ)
    yup, ydn = lax.rem(gy + 1, NGY), lax.rem(gy + NGY - 1, NGY)
    lane = lane_index()
    first, last = lane == 0, lane == LANES - 1

    barrier = pltpu.get_barrier_semaphore()
    partners = [(gz, yup), (gz, ydn), (zup, yup), (zup, ydn), (zdn, yup), (zdn, ydn)]
    partners += [(lax.rem(gz + d, NGZ), gy) for d in range(1, NGZ)]
    for a, b in partners:
        pl.semaphore_signal(barrier, inc=1, device_id=(a, b), device_id_type=MESH)

    srcs = (t_hbm, u_hbm, v_hbm, w_hbm)
    for f in range(4):
        for h in range(2):
            for x in range(NX):
                pltpu.make_async_copy(
                    srcs[f].at[x, :, pl.ds(h * LANES, LANES)],
                    s0.at[f, h, pl.ds(2, NY), x, :],
                    in_sem.at[f],
                ).start()
    for h in range(2):
        for x in range(NX):
            pltpu.make_async_copy(
                m_hbm.at[x, :, pl.ds(h * LANES, LANES)],
                mk.at[h, pl.ds(1, NY), x, :],
                in_sem.at[4],
            ).start()

    zero = jnp.zeros((NX, LANES), F32)
    low2 = (lane & 3) < 2
    left = lane < LANES // 2

    def pack(f, load):
        def body(k, carry):
            groups = []
            for g in range(4):
                acc = None
                for j in range(8 * g, 8 * g + 8):
                    y = 4 * j + k
                    both = jnp.where(left, load(0, y), load(1, y))
                    r = pltpu.roll(both, (4 * j + 2) % LANES, 1)
                    acc = r if acc is None else jnp.where(lane >= 4 * j, r, acc)
                groups.append(acc)
            a = jnp.where(lane >= 32, groups[1], groups[0])
            b = jnp.where(lane >= 96, groups[3], groups[2])
            own[f, k] = jnp.where(lane >= 64, b, a).astype(F32)
            return carry

        lax.fori_loop(0, 4, body, 0)

    corner_l, corner_r = zero, zero
    for f in range(4):
        whole = s0.at[f, :, pl.ds(2, NY), :, :]
        pltpu.make_async_copy(whole, whole, in_sem.at[f]).wait()
        pack(f, lambda h, y, f=f: s0[f, h, y + 2])
        corner_l = jnp.where(lane == f, pltpu.roll(s0[f, 0, 2], f, 1), corner_l)
        corner_l = jnp.where(lane == 124 + f, pltpu.roll(s0[f, 0, NY + 1], 124 + f, 1), corner_l)
        corner_r = jnp.where(lane == f, pltpu.roll(s0[f, 1, 2], f + 1, 1), corner_r)
        corner_r = jnp.where(lane == 124 + f, pltpu.roll(s0[f, 1, NY + 1], (125 + f) % LANES, 1), corner_r)
    whole = mk.at[:, pl.ds(1, NY), :, :]
    pltpu.make_async_copy(whole, whole, in_sem.at[4]).wait()
    pack(4, lambda h, y: mk[h, y + 1])
    for f in range(5):
        for p in range(2):
            even, odd = own[f, 2 * p], own[f, 2 * p + 1]
            zsrc[0, f, p] = jnp.where(low2, pltpu.roll(even, LANES - 2, 1), odd)
            zsrc[1, f, p] = jnp.where(low2, even, pltpu.roll(odd, 2, 1))
    corner[0] = corner_l
    corner[1] = corner_r

    pl.semaphore_wait(barrier, len(partners))

    def remote(src, dst, ssem, rsem, dev):
        return pltpu.make_async_remote_copy(
            src_ref=src, dst_ref=dst, send_sem=ssem, recv_sem=rsem,
            device_id=dev, device_id_type=MESH,
        )

    z_copies = [
        remote(zsrc.at[0], got.at[1], zsend.at[0], zrecv.at[0], (zdn, gy)),
        remote(zsrc.at[1], got.at[0], zsend.at[1], zrecv.at[1], (zup, gy)),
    ]
    c_copies = [
        remote(corner.at[0], got_corner.at[1, 1], csend.at[0], crecv.at[0], (zdn, ydn)),
        remote(corner.at[0], got_corner.at[1, 0], csend.at[1], crecv.at[1], (zdn, yup)),
        remote(corner.at[1], got_corner.at[0, 1], csend.at[2], crecv.at[2], (zup, ydn)),
        remote(corner.at[1], got_corner.at[0, 0], csend.at[3], crecv.at[3], (zup, yup)),
    ]
    y_copies = [
        remote(s0.at[:, :, pl.ds(2, 2)], s0.at[:, :, pl.ds(NY + 2, 2)], ysend.at[0], yrecv.at[0], (gz, ydn)),
        remote(s0.at[:, :, pl.ds(NY, 2)], s0.at[:, :, pl.ds(0, 2)], ysend.at[1], yrecv.at[1], (gz, yup)),
        remote(mk.at[:, 1], mk.at[:, NY + 1], ysend.at[2], yrecv.at[2], (gz, ydn)),
        remote(mk.at[:, NY], mk.at[:, 0], ysend.at[3], yrecv.at[3], (gz, yup)),
    ]
    for cp in z_copies + c_copies + y_copies:
        cp.start()
    bottom, top = gz == 0, gz == NGZ - 1

    def rows(src, j, below, above):
        halves = []
        ca = [src[f, 0, j] for f in range(4)]
        cb = [src[f, 1, j] for f in range(4)]
        ap = [pltpu.roll(v, 1, 1) for v in ca]
        bp = [pltpu.roll(v, 1, 1) for v in cb]
        am = [pltpu.roll(v, LANES - 1, 1) for v in ca]
        bm = [pltpu.roll(v, LANES - 1, 1) for v in cb]
        for h, c in ((0, ca), (1, cb)):
            if h == 0:
                lo = ap if below is None else [jnp.where(first, below[f], ap[f]) for f in range(4)]
                up = [jnp.where(last, bm[f], am[f]) for f in range(4)]
            else:
                lo = [jnp.where(first, ap[f], bp[f]) for f in range(4)]
                up = bm if above is None else [jnp.where(last, above[f], bm[f]) for f in range(4)]
            ew = [around_x(v) for v in c]
            n = [src[f, h, j + 1] for f in range(4)]
            s = [src[f, h, j - 1] for f in range(4)]
            halves.append(advance(c, [p[0] for p in ew], [p[1] for p in ew], n, s, up, lo))
        return ca, cb, halves

    def row_one(y, ends):
        below, above = ends
        halves = rows(s0, y + 2, below, above)[2]
        for h in range(2):
            m = mk[h, y + 1].astype(F32)
            s1[0, h, y + 1] = halves[h][0]
            for f in range(1, 4):
                s1[f, h, y + 1] = halves[h][f] * m

    def loop_one(y, carry):
        row_one(y, (None, None))
        return carry

    lax.fori_loop(1, NY - 1, loop_one, 0, unroll=UNROLL)

    for cp in z_copies + c_copies + y_copies:
        cp.wait()
    loop_one(0, 0)
    loop_one(NY - 1, 0)

    ends = []
    for side in range(2):
        for f in range(4):
            lo = pltpu.roll(got_corner[side, 0], (3 - f) % LANES, 1)
            hi = pltpu.roll(got_corner[side, 1], (LANES - f) % LANES, 1)
            v = jnp.where(last, lo, hi)
            ends.append(jnp.where(bottom if side == 0 else top, 0.0, v))
    end_of = lambda side, f: ends[side * 4 + f]

    row_one(-1, (
        [pltpu.roll(end_of(0, f), 1, 1) for f in range(4)],
        [end_of(1, f) for f in range(4)],
    ))
    row_one(NY, (
        [end_of(0, f) for f in range(4)],
        [pltpu.roll(end_of(1, f), LANES - 1, 1) for f in range(4)],
    ))
    for side in range(2):
        for f in range(5):
            for k in range(4):
                g = got[side, f, k // 2]
                if side == 0 and k % 2 == 1:
                    g = pltpu.roll(g, LANES - 2, 1)
                if side == 1 and k % 2 == 0:
                    g = pltpu.roll(g, 2, 1)
                if f < 4:
                    g = jnp.where(bottom if side == 0 else top, 0.0, g)
                near = own[f, k]
                merged[side, f, k + 1] = jnp.where(low2, g, near) if side == 0 else jnp.where(low2, near, g)
        for f in range(4):
            end = end_of(side, f)
            before = jnp.where(lane == 1 + side, pltpu.roll(end, 2 + side, 1), pltpu.roll(s0[f, side, 1], 2, 1))
            after = jnp.where(
                lane == 125 + side, pltpu.roll(end, 125 + side, 1), pltpu.roll(s0[f, side, NY + 2], 126, 1)
            )
            merged[side, f, 0] = jnp.where(lane < 4, before, pltpu.roll(merged[side, f, 4], 4, 1))
            merged[side, f, 5] = jnp.where(lane >= 124, after, pltpu.roll(merged[side, f, 1], 124, 1))

        def edge(k, carry, side=side):
            c = [merged[side, f, k + 1] for f in range(4)]
            n = [merged[side, f, k + 2] for f in range(4)]
            s = [merged[side, f, k] for f in range(4)]
            lo = [pltpu.roll(v, 1, 1) for v in c]
            up = [pltpu.roll(v, LANES - 1, 1) for v in c]
            ew = [around_x(v) for v in c]
            new = advance(c, [p[0] for p in ew], [p[1] for p in ew], n, s, up, lo)
            m = merged[side, 4, k + 1]
            for f in range(4):
                edges[side, f, k] = new[f] if f == 0 else new[f] * m
            return carry

        lax.fori_loop(0, 4, edge, 0, unroll=2)

    def unpack(k, carry):
        for f in range(4):
            b, t = edges[0, f, k], edges[1, f, k]
            inner = jnp.where(low2, t, b)
            outer = jnp.where(
                low2,
                jnp.where(top, 0.0, pltpu.roll(t, LANES - 1, 1)),
                jnp.where(bottom, 0.0, pltpu.roll(b, 1, 1)),
            )
            for j in range(32):
                y = 4 * j + k
                shift = (2 * LANES - 4 * j - 2) % LANES
                v = pltpu.roll(inner, shift, 1)
                s1[f, 0, y + 1] = jnp.where(first, v, s1[f, 0, y + 1])
                s1[f, 1, y + 1] = jnp.where(last, v, s1[f, 1, y + 1])
                ring[f, y] = pltpu.roll(outer, shift, 1)
        return carry

    lax.fori_loop(0, 4, unpack, 0)

    def loop_two(y, acc):
        past = [ring[f, y] for f in range(4)]
        halves = rows(s1, y + 1, past, past)[2]
        total = None
        for h in range(2):
            m = 0.5 * mk[h, y + 1].astype(F32)
            for f in range(4):
                v = s0[f, h, y + 2] + halves[h][f]
                v = 0.5 * v if f == 0 else v * m
                res[f, h, y] = v
                if f == 0:
                    r = 1.0 - jnp.exp(-0.125 * v)
                    total = r if total is None else total + r
        return jnp.where(lane == y, jnp.sum(total, axis=1, keepdims=True), acc)

    acc = lax.fori_loop(0, NY, loop_two, zero, unroll=UNROLL)

    part[...] = acc
    copies = []
    for d in range(1, NGZ):
        peer = lax.rem(gz + d, NGZ)
        copies.append(remote(
            part.at[pl.ds(peer, 1)], got_part.at[d - 1], psend.at[d - 1], precv.at[d - 1], (peer, gy),
        ))
    for cp in copies:
        cp.start()
    total = part[pl.ds(gz, 1)]
    for cp in copies:
        cp.wait()
    for d in range(NGZ - 1):
        total = total + got_part[d]
    path[...] = total * (8.0 / math.sqrt(2048.0))


def emit(res, path, t_out, u_out, v_out, w_out, path_out, out_sem):
    outs = (t_out, u_out, v_out, w_out)
    for f in range(4):
        for h in range(2):
            for x in range(NX):
                pltpu.make_async_copy(
                    res.at[f, h, :, x, :],
                    outs[f].at[x, :, pl.ds(h * LANES, LANES)],
                    out_sem.at[f],
                ).start()
    path_out[...] = path[...]
    for f in range(4):
        whole = res.at[f]
        pltpu.make_async_copy(whole, whole, out_sem.at[f]).wait()


def on_device(*args):
    block = jax.ShapeDtypeStruct((NX, NY, 2 * LANES), F32)
    line = jax.ShapeDtypeStruct((1, NY), F32)
    anywhere = pl.BlockSpec(memory_space=pl.ANY)
    inside = pl.BlockSpec(memory_space=pltpu.VMEM)
    res, path = pl.pallas_call(
        kernel,
        out_shape=(pltpu.VMEM((4, 2, NY, NX, LANES), F32), pltpu.VMEM((1, NY), F32)),
        in_specs=[anywhere] * 5,
        out_specs=(inside, inside),
        scratch_shapes=[
            pltpu.VMEM((4, 2, NY + 4, NX, LANES), F32),
            pltpu.VMEM((4, 2, NY + 2, NX, LANES), F32),
            pltpu.VMEM((2, NY + 2, NX, LANES), jnp.int32),
            pltpu.VMEM((5, 4, NX, LANES), F32),
            pltpu.VMEM((2, 5, 2, NX, LANES), F32),
            pltpu.VMEM((2, 5, 2, NX, LANES), F32),
            pltpu.VMEM((2, 5, 6, NX, LANES), F32),
            pltpu.VMEM((2, 4, 4, NX, LANES), F32),
            pltpu.VMEM((2, NX, LANES), F32),
            pltpu.VMEM((2, 2, NX, LANES), F32),
            pltpu.VMEM((4, NY, NX, LANES), F32),
            pltpu.VMEM((NX, LANES), F32),
            pltpu.VMEM((NGZ - 1, 1, LANES), F32),
            pltpu.SemaphoreType.DMA((5,)),
            pltpu.SemaphoreType.DMA((4,)),
            pltpu.SemaphoreType.DMA((4,)),
            pltpu.SemaphoreType.DMA((2,)),
            pltpu.SemaphoreType.DMA((2,)),
            pltpu.SemaphoreType.DMA((4,)),
            pltpu.SemaphoreType.DMA((4,)),
            pltpu.SemaphoreType.DMA((NGZ - 1,)),
            pltpu.SemaphoreType.DMA((NGZ - 1,)),
        ],
        compiler_params=pltpu.CompilerParams(
            collective_id=0, has_side_effects=True, vmem_limit_bytes=59 * 1024 * 1024
        ),
        name="flow",
    )(*args)
    return pl.pallas_call(
        emit,
        out_shape=(block, block, block, block, line),
        in_specs=[inside, inside],
        out_specs=(anywhere,) * 4 + (inside,),
        scratch_shapes=[pltpu.SemaphoreType.DMA((4,))],
        compiler_params=pltpu.CompilerParams(vmem_limit_bytes=8 * 1024 * 1024),
        name="emit",
    )(res, path)


def solution(mesh):
    split = P(None, "gy", "gz")
    return jax.shard_map(
        on_device,
        mesh=mesh,
        in_specs=(split,) * 5,
        out_specs=(split,) * 4 + (P("gz", "gy"),),
        check_vma=False,
    )
```

```python
import math

import jax
import jax.numpy as jnp
from jax import lax
from jax.experimental import pallas as pl
from jax.experimental.pallas import tpu as pltpu
from jax.sharding import PartitionSpec as P

MESH = pl.DeviceIdType.MESH
NX, NY, LANES = 8, 128, 128
NGZ, NGY = 8, 16
UNROLL = 3
ROWS = 4
F32 = jnp.float32


def lane_index():
    return lax.broadcasted_iota(jnp.int32, (NX, LANES), 1)


def advance(c, e, w, n, s, u, l):
    dx = [e[i] - w[i] for i in range(4)]
    dy = [n[i] - s[i] for i in range(4)]
    dz = [u[i] - l[i] for i in range(4)]
    shear_a = dy[1] + dx[2]
    shear_b = dz[1] + dx[3]
    shear_c = dz[2] + dy[3]
    normal = dx[1] * dx[1] + dy[2] * dy[2] + dz[3] * dz[3]
    shear = shear_a * shear_a + shear_b * shear_b + shear_c * shear_c
    arg = 4.5e-6 * normal + 2.25e-6 * shear + 9e-8
    eddy = arg * lax.rsqrt(arg)
    k_vel = eddy + 0.005
    k_heat = 2.5 * eddy + 0.005
    rest_vel = 1.0 - 6.0 * k_vel
    rest_heat = 1.0 - 6.0 * k_heat
    au = -0.05 * c[1]
    av = -0.05 * c[2]
    aw = -0.05 * c[3]
    out = []
    for i in range(4):
        around = (e[i] + w[i]) + (n[i] + s[i]) + (u[i] + l[i])
        k, rest = (k_heat, rest_heat) if i == 0 else (k_vel, rest_vel)
        out.append(k * around + rest * c[i] + (au * dx[i] + av * dy[i] + aw * dz[i]))
    out[3] = out[3] + 0.05 * c[0]
    return out


def around_x(v):
    return pltpu.roll(v, NX - 1, 0), pltpu.roll(v, 1, 0)


def kernel(
    t_hbm, u_hbm, v_hbm, w_hbm, m_hbm,
    res, path,
    s0, s1, mk, own, zsrc, got, merged, edges, corner, got_corner, ring, part, got_part,
    in_sem, ysend, yrecv, zsend, zrecv, csend, crecv, psend, precv,
):
    gz = lax.axis_index("gz")
    gy = lax.axis_index("gy")
    zup, zdn = lax.rem(gz + 1, NGZ), lax.rem(gz + NGZ - 1, NGZ)
    yup, ydn = lax.rem(gy + 1, NGY), lax.rem(gy + NGY - 1, NGY)
    lane = lane_index()
    first, last = lane == 0, lane == LANES - 1

    barrier = pltpu.get_barrier_semaphore()
    partners = [(gz, yup), (gz, ydn), (zup, yup), (zup, ydn), (zdn, yup), (zdn, ydn)]
    partners += [(lax.rem(gz + d, NGZ), gy) for d in range(1, NGZ)]
    for a, b in partners:
        pl.semaphore_signal(barrier, inc=1, device_id=(a, b), device_id_type=MESH)

    srcs = (t_hbm, u_hbm, v_hbm, w_hbm)
    for f in range(4):
        for h in range(2):
            for x in range(NX):
                pltpu.make_async_copy(
                    srcs[f].at[x, :, pl.ds(h * LANES, LANES)],
                    s0.at[f, h, pl.ds(2, NY), x, :],
                    in_sem.at[f],
                ).start()
    for h in range(2):
        for x in range(NX):
            pltpu.make_async_copy(
                m_hbm.at[x, :, pl.ds(h * LANES, LANES)],
                mk.at[h, pl.ds(1, NY), x, :],
                in_sem.at[4],
            ).start()

    zero = jnp.zeros((NX, LANES), F32)
    low2 = (lane & 3) < 2
    left = lane < LANES // 2

    def pack(f, load):
        def body(k, carry):
            groups = []
            for g in range(4):
                acc = None
                for j in range(8 * g, 8 * g + 8):
                    y = 4 * j + k
                    both = jnp.where(left, load(0, y), load(1, y))
                    r = pltpu.roll(both, (4 * j + 2) % LANES, 1)
                    acc = r if acc is None else jnp.where(lane >= 4 * j, r, acc)
                groups.append(acc)
            a = jnp.where(lane >= 32, groups[1], groups[0])
            b = jnp.where(lane >= 96, groups[3], groups[2])
            own[f, k] = jnp.where(lane >= 64, b, a).astype(F32)
            return carry

        lax.fori_loop(0, 4, body, 0, unroll=2)

    corner_l, corner_r = zero, zero
    for f in range(4):
        whole = s0.at[f, :, pl.ds(2, NY), :, :]
        pltpu.make_async_copy(whole, whole, in_sem.at[f]).wait()
        pack(f, lambda h, y, f=f: s0[f, h, y + 2])
        corner_l = jnp.where(lane == f, pltpu.roll(s0[f, 0, 2], f, 1), corner_l)
        corner_l = jnp.where(lane == 124 + f, pltpu.roll(s0[f, 0, NY + 1], 124 + f, 1), corner_l)
        corner_r = jnp.where(lane == f, pltpu.roll(s0[f, 1, 2], f + 1, 1), corner_r)
        corner_r = jnp.where(lane == 124 + f, pltpu.roll(s0[f, 1, NY + 1], (125 + f) % LANES, 1), corner_r)
    whole = mk.at[:, pl.ds(1, NY), :, :]
    pltpu.make_async_copy(whole, whole, in_sem.at[4]).wait()
    pack(4, lambda h, y: mk[h, y + 1])
    for f in range(5):
        for p in range(2):
            even, odd = own[f, 2 * p], own[f, 2 * p + 1]
            zsrc[0, f, p] = jnp.where(low2, pltpu.roll(even, LANES - 2, 1), odd)
            zsrc[1, f, p] = jnp.where(low2, even, pltpu.roll(odd, 2, 1))
    corner[0] = corner_l
    corner[1] = corner_r

    pl.semaphore_wait(barrier, len(partners))

    def remote(src, dst, ssem, rsem, dev):
        return pltpu.make_async_remote_copy(
            src_ref=src, dst_ref=dst, send_sem=ssem, recv_sem=rsem,
            device_id=dev, device_id_type=MESH,
        )

    z_copies = [
        remote(zsrc.at[0], got.at[1], zsend.at[0], zrecv.at[0], (zdn, gy)),
        remote(zsrc.at[1], got.at[0], zsend.at[1], zrecv.at[1], (zup, gy)),
    ]
    c_copies = [
        remote(corner.at[0], got_corner.at[1, 1], csend.at[0], crecv.at[0], (zdn, ydn)),
        remote(corner.at[0], got_corner.at[1, 0], csend.at[1], crecv.at[1], (zdn, yup)),
        remote(corner.at[1], got_corner.at[0, 1], csend.at[2], crecv.at[2], (zup, ydn)),
        remote(corner.at[1], got_corner.at[0, 0], csend.at[3], crecv.at[3], (zup, yup)),
    ]
    y_copies = [
        remote(s0.at[:, :, pl.ds(2, 2)], s0.at[:, :, pl.ds(NY + 2, 2)], ysend.at[0], yrecv.at[0], (gz, ydn)),
        remote(s0.at[:, :, pl.ds(NY, 2)], s0.at[:, :, pl.ds(0, 2)], ysend.at[1], yrecv.at[1], (gz, yup)),
        remote(mk.at[:, 1], mk.at[:, NY + 1], ysend.at[2], yrecv.at[2], (gz, ydn)),
        remote(mk.at[:, NY], mk.at[:, 0], ysend.at[3], yrecv.at[3], (gz, yup)),
    ]
    for cp in z_copies + c_copies + y_copies:
        cp.start()
    bottom, top = gz == 0, gz == NGZ - 1

    def rows(src, j, below, above):
        halves = []
        ca = [src[f, 0, j] for f in range(4)]
        cb = [src[f, 1, j] for f in range(4)]
        ap = [pltpu.roll(v, 1, 1) for v in ca]
        bp = [pltpu.roll(v, 1, 1) for v in cb]
        am = [pltpu.roll(v, LANES - 1, 1) for v in ca]
        bm = [pltpu.roll(v, LANES - 1, 1) for v in cb]
        for h, c in ((0, ca), (1, cb)):
            if h == 0:
                lo = ap if below is None else [jnp.where(first, below[f], ap[f]) for f in range(4)]
                up = [jnp.where(last, bm[f], am[f]) for f in range(4)]
            else:
                lo = [jnp.where(first, ap[f], bp[f]) for f in range(4)]
                up = bm if above is None else [jnp.where(last, above[f], bm[f]) for f in range(4)]
            ew = [around_x(v) for v in c]
            n = [src[f, h, j + 1] for f in range(4)]
            s = [src[f, h, j - 1] for f in range(4)]
            halves.append(advance(c, [p[0] for p in ew], [p[1] for p in ew], n, s, up, lo))
        return ca, cb, halves

    def row_one(y, ends):
        below, above = ends
        halves = rows(s0, y + 2, below, above)[2]
        for h in range(2):
            m = mk[h, y + 1].astype(F32)
            s1[0, h, y + 1] = halves[h][0]
            for f in range(1, 4):
                s1[f, h, y + 1] = halves[h][f] * m

    def loop_one(y, carry):
        row_one(y, (None, None))
        return carry

    lax.fori_loop(1, NY - 1, loop_one, 0, unroll=UNROLL)

    for cp in z_copies + c_copies + y_copies:
        cp.wait()
    loop_one(0, 0)
    loop_one(NY - 1, 0)

    ends = []
    for side in range(2):
        for f in range(4):
            lo = pltpu.roll(got_corner[side, 0], (3 - f) % LANES, 1)
            hi = pltpu.roll(got_corner[side, 1], (LANES - f) % LANES, 1)
            v = jnp.where(last, lo, hi)
            ends.append(jnp.where(bottom if side == 0 else top, 0.0, v))
    end_of = lambda side, f: ends[side * 4 + f]

    row_one(-1, (
        [pltpu.roll(end_of(0, f), 1, 1) for f in range(4)],
        [end_of(1, f) for f in range(4)],
    ))
    row_one(NY, (
        [end_of(0, f) for f in range(4)],
        [pltpu.roll(end_of(1, f), LANES - 1, 1) for f in range(4)],
    ))
    for side in range(2):
        for f in range(5):
            for k in range(4):
                g = got[side, f, k // 2]
                if side == 0 and k % 2 == 1:
                    g = pltpu.roll(g, LANES - 2, 1)
                if side == 1 and k % 2 == 0:
                    g = pltpu.roll(g, 2, 1)
                if f < 4:
                    g = jnp.where(bottom if side == 0 else top, 0.0, g)
                near = own[f, k]
                merged[side, f, k + 1] = jnp.where(low2, g, near) if side == 0 else jnp.where(low2, near, g)
        for f in range(4):
            end = end_of(side, f)
            before = jnp.where(lane == 1 + side, pltpu.roll(end, 2 + side, 1), pltpu.roll(s0[f, side, 1], 2, 1))
            after = jnp.where(
                lane == 125 + side, pltpu.roll(end, 125 + side, 1), pltpu.roll(s0[f, side, NY + 2], 126, 1)
            )
            merged[side, f, 0] = jnp.where(lane < 4, before, pltpu.roll(merged[side, f, 4], 4, 1))
            merged[side, f, 5] = jnp.where(lane >= 124, after, pltpu.roll(merged[side, f, 1], 124, 1))

        def edge(k, carry, side=side):
            c = [merged[side, f, k + 1] for f in range(4)]
            n = [merged[side, f, k + 2] for f in range(4)]
            s = [merged[side, f, k] for f in range(4)]
            lo = [pltpu.roll(v, 1, 1) for v in c]
            up = [pltpu.roll(v, LANES - 1, 1) for v in c]
            ew = [around_x(v) for v in c]
            new = advance(c, [p[0] for p in ew], [p[1] for p in ew], n, s, up, lo)
            m = merged[side, 4, k + 1]
            for f in range(4):
                edges[side, f, k] = new[f] if f == 0 else new[f] * m
            return carry

        lax.fori_loop(0, 4, edge, 0, unroll=2)

    def unpack(k, carry):
        for f in range(4):
            b, t = edges[0, f, k], edges[1, f, k]
            inner = jnp.where(low2, t, b)
            outer = jnp.where(
                low2,
                jnp.where(top, 0.0, pltpu.roll(t, LANES - 1, 1)),
                jnp.where(bottom, 0.0, pltpu.roll(b, 1, 1)),
            )
            for j in range(32):
                y = 4 * j + k
                shift = (2 * LANES - 4 * j - 2) % LANES
                v = pltpu.roll(inner, shift, 1)
                s1[f, 0, y + 1] = jnp.where(first, v, s1[f, 0, y + 1])
                s1[f, 1, y + 1] = jnp.where(last, v, s1[f, 1, y + 1])
                ring[f, y] = pltpu.roll(outer, shift, 1)
        return carry

    lax.fori_loop(0, 4, unpack, 0)

    def row_sum(y, pair, acc):
        total = (1.0 - jnp.exp(-0.125 * pair[0])) + (1.0 - jnp.exp(-0.125 * pair[1]))
        return jnp.where(lane == y, jnp.sum(total, axis=1, keepdims=True), acc)

    def loop_two(i, carry):
        acc, warm = carry
        y0 = i * ROWS
        new = []
        for r in range(ROWS):
            y = y0 + r
            past = [ring[f, y] for f in range(4)]
            halves = rows(s1, y + 1, past, past)[2]
            pair = []
            for h in range(2):
                m = 0.5 * mk[h, y + 1].astype(F32)
                for f in range(4):
                    v = s0[f, h, y + 2] + halves[h][f]
                    v = 0.5 * v if f == 0 else v * m
                    res[f, h, y] = v
                    if f == 0:
                        pair.append(v)
            new.append(tuple(pair))
        for r in range(ROWS):
            acc = row_sum(y0 + r - ROWS, warm[r], acc)
        return acc, tuple(new)

    res[0, 0, 0] = zero
    blank = res[0, 0, 0]
    acc, warm = lax.fori_loop(0, NY // ROWS, loop_two, (blank, ((blank, blank),) * ROWS))
    for r in range(ROWS):
        acc = row_sum(NY - ROWS + r, warm[r], acc)

    part[...] = acc
    copies = []
    for d in range(1, NGZ):
        peer = lax.rem(gz + d, NGZ)
        copies.append(remote(
            part.at[pl.ds(peer, 1)], got_part.at[d - 1], psend.at[d - 1], precv.at[d - 1], (peer, gy),
        ))
    for cp in copies:
        cp.start()
    total = part[pl.ds(gz, 1)]
    for cp in copies:
        cp.wait()
    for d in range(NGZ - 1):
        total = total + got_part[d]
    path[...] = total * (8.0 / math.sqrt(2048.0))


def emit(res, path, t_out, u_out, v_out, w_out, path_out, out_sem):
    outs = (t_out, u_out, v_out, w_out)
    for f in range(4):
        for h in range(2):
            for x in range(NX):
                pltpu.make_async_copy(
                    res.at[f, h, :, x, :],
                    outs[f].at[x, :, pl.ds(h * LANES, LANES)],
                    out_sem.at[f],
                ).start()
    path_out[...] = path[...]
    for f in range(4):
        whole = res.at[f]
        pltpu.make_async_copy(whole, whole, out_sem.at[f]).wait()


def on_device(*args):
    block = jax.ShapeDtypeStruct((NX, NY, 2 * LANES), F32)
    line = jax.ShapeDtypeStruct((1, NY), F32)
    anywhere = pl.BlockSpec(memory_space=pl.ANY)
    inside = pl.BlockSpec(memory_space=pltpu.VMEM)
    res, path = pl.pallas_call(
        kernel,
        out_shape=(pltpu.VMEM((4, 2, NY, NX, LANES), F32), pltpu.VMEM((1, NY), F32)),
        in_specs=[anywhere] * 5,
        out_specs=(inside, inside),
        scratch_shapes=[
            pltpu.VMEM((4, 2, NY + 4, NX, LANES), F32),
            pltpu.VMEM((4, 2, NY + 2, NX, LANES), F32),
            pltpu.VMEM((2, NY + 2, NX, LANES), jnp.int32),
            pltpu.VMEM((5, 4, NX, LANES), F32),
            pltpu.VMEM((2, 5, 2, NX, LANES), F32),
            pltpu.VMEM((2, 5, 2, NX, LANES), F32),
            pltpu.VMEM((2, 5, 6, NX, LANES), F32),
            pltpu.VMEM((2, 4, 4, NX, LANES), F32),
            pltpu.VMEM((2, NX, LANES), F32),
            pltpu.VMEM((2, 2, NX, LANES), F32),
            pltpu.VMEM((4, NY, NX, LANES), F32),
            pltpu.VMEM((NX, LANES), F32),
            pltpu.VMEM((NGZ - 1, 1, LANES), F32),
            pltpu.SemaphoreType.DMA((5,)),
            pltpu.SemaphoreType.DMA((4,)),
            pltpu.SemaphoreType.DMA((4,)),
            pltpu.SemaphoreType.DMA((2,)),
            pltpu.SemaphoreType.DMA((2,)),
            pltpu.SemaphoreType.DMA((4,)),
            pltpu.SemaphoreType.DMA((4,)),
            pltpu.SemaphoreType.DMA((NGZ - 1,)),
            pltpu.SemaphoreType.DMA((NGZ - 1,)),
        ],
        compiler_params=pltpu.CompilerParams(
            collective_id=0, has_side_effects=True, vmem_limit_bytes=59 * 1024 * 1024
        ),
        name="flow",
    )(*args)
    return pl.pallas_call(
        emit,
        out_shape=(block, block, block, block, line),
        in_specs=[inside, inside],
        out_specs=(anywhere,) * 4 + (inside,),
        scratch_shapes=[pltpu.SemaphoreType.DMA((4,))],
        compiler_params=pltpu.CompilerParams(vmem_limit_bytes=8 * 1024 * 1024),
        name="emit",
    )(res, path)


def solution(mesh):
    split = P(None, "gy", "gz")
    return jax.shard_map(
        on_device,
        mesh=mesh,
        in_specs=(split,) * 5,
        out_specs=(split,) * 4 + (P("gz", "gy"),),
        check_vma=False,
    )
```

```python
import math

import jax
import jax.numpy as jnp
from jax import lax
from jax.experimental import pallas as pl
from jax.experimental.pallas import tpu as pltpu
from jax.sharding import PartitionSpec as P

MESH = pl.DeviceIdType.MESH
NX, NY, LANES = 8, 128, 128
NGZ, NGY = 8, 16
UNROLL = 3
ROWS = 4
F32 = jnp.float32


def lane_index():
    return lax.broadcasted_iota(jnp.int32, (NX, LANES), 1)


def advance(c, e, w, n, s, u, l):
    dx = [e[i] - w[i] for i in range(4)]
    dy = [n[i] - s[i] for i in range(4)]
    dz = [u[i] - l[i] for i in range(4)]
    shear_a = dy[1] + dx[2]
    shear_b = dz[1] + dx[3]
    shear_c = dz[2] + dy[3]
    normal = dx[1] * dx[1] + dy[2] * dy[2] + dz[3] * dz[3]
    shear = shear_a * shear_a + shear_b * shear_b + shear_c * shear_c
    arg = 4.5e-6 * normal + 2.25e-6 * shear + 9e-8
    eddy = arg * lax.rsqrt(arg)
    k_vel = eddy + 0.005
    k_heat = 2.5 * eddy + 0.005
    rest_vel = 1.0 - 6.0 * k_vel
    rest_heat = 1.0 - 6.0 * k_heat
    au = -0.05 * c[1]
    av = -0.05 * c[2]
    aw = -0.05 * c[3]
    out = []
    for i in range(4):
        around = (e[i] + w[i]) + (n[i] + s[i]) + (u[i] + l[i])
        k, rest = (k_heat, rest_heat) if i == 0 else (k_vel, rest_vel)
        out.append(k * around + rest * c[i] + (au * dx[i] + av * dy[i] + aw * dz[i]))
    out[3] = out[3] + 0.05 * c[0]
    return out


def around_x(v):
    return pltpu.roll(v, NX - 1, 0), pltpu.roll(v, 1, 0)


def kernel(
    t_hbm, u_hbm, v_hbm, w_hbm, m_hbm,
    res, path,
    s0, s1, mk, own, zsrc, got, merged, edges, corner, got_corner, ring, part, got_part,
    in_sem, ysend, yrecv, zsend, zrecv, csend, crecv, psend, precv,
):
    gz = lax.axis_index("gz")
    gy = lax.axis_index("gy")
    zup, zdn = lax.rem(gz + 1, NGZ), lax.rem(gz + NGZ - 1, NGZ)
    yup, ydn = lax.rem(gy + 1, NGY), lax.rem(gy + NGY - 1, NGY)
    lane = lane_index()
    first, last = lane == 0, lane == LANES - 1

    barrier = pltpu.get_barrier_semaphore()
    partners = [(gz, yup), (gz, ydn), (zup, yup), (zup, ydn), (zdn, yup), (zdn, ydn)]
    partners += [(lax.rem(gz + d, NGZ), gy) for d in range(1, NGZ)]
    for a, b in partners:
        pl.semaphore_signal(barrier, inc=1, device_id=(a, b), device_id_type=MESH)

    srcs = (t_hbm, u_hbm, v_hbm, w_hbm)
    for f in range(4):
        for h in range(2):
            for x in range(NX):
                pltpu.make_async_copy(
                    srcs[f].at[x, :, pl.ds(h * LANES, LANES)],
                    s0.at[f, h, pl.ds(2, NY), x, :],
                    in_sem.at[f],
                ).start()
    for h in range(2):
        for x in range(NX):
            pltpu.make_async_copy(
                m_hbm.at[x, :, pl.ds(h * LANES, LANES)],
                mk.at[h, pl.ds(1, NY), x, :],
                in_sem.at[4],
            ).start()

    zero = jnp.zeros((NX, LANES), F32)
    low2 = (lane & 3) < 2
    left = lane < LANES // 2

    def pack(f, load):
        def body(k, carry):
            groups = []
            for g in range(4):
                acc = None
                for j in range(8 * g, 8 * g + 8):
                    y = 4 * j + k
                    both = jnp.where(left, load(0, y), load(1, y))
                    r = pltpu.roll(both, (4 * j + 2) % LANES, 1)
                    acc = r if acc is None else jnp.where(lane >= 4 * j, r, acc)
                groups.append(acc)
            a = jnp.where(lane >= 32, groups[1], groups[0])
            b = jnp.where(lane >= 96, groups[3], groups[2])
            own[f, k] = jnp.where(lane >= 64, b, a).astype(F32)
            return carry

        lax.fori_loop(0, 4, body, 0, unroll=4)

    corner_l, corner_r = zero, zero
    for f in range(4):
        whole = s0.at[f, :, pl.ds(2, NY), :, :]
        pltpu.make_async_copy(whole, whole, in_sem.at[f]).wait()
        pack(f, lambda h, y, f=f: s0[f, h, y + 2])
        corner_l = jnp.where(lane == f, pltpu.roll(s0[f, 0, 2], f, 1), corner_l)
        corner_l = jnp.where(lane == 124 + f, pltpu.roll(s0[f, 0, NY + 1], 124 + f, 1), corner_l)
        corner_r = jnp.where(lane == f, pltpu.roll(s0[f, 1, 2], f + 1, 1), corner_r)
        corner_r = jnp.where(lane == 124 + f, pltpu.roll(s0[f, 1, NY + 1], (125 + f) % LANES, 1), corner_r)
    whole = mk.at[:, pl.ds(1, NY), :, :]
    pltpu.make_async_copy(whole, whole, in_sem.at[4]).wait()
    pack(4, lambda h, y: mk[h, y + 1])
    for f in range(5):
        for p in range(2):
            even, odd = own[f, 2 * p], own[f, 2 * p + 1]
            zsrc[0, f, p] = jnp.where(low2, pltpu.roll(even, LANES - 2, 1), odd)
            zsrc[1, f, p] = jnp.where(low2, even, pltpu.roll(odd, 2, 1))
    corner[0] = corner_l
    corner[1] = corner_r

    pl.semaphore_wait(barrier, len(partners))

    def remote(src, dst, ssem, rsem, dev):
        return pltpu.make_async_remote_copy(
            src_ref=src, dst_ref=dst, send_sem=ssem, recv_sem=rsem,
            device_id=dev, device_id_type=MESH,
        )

    z_copies = [
        remote(zsrc.at[0], got.at[1], zsend.at[0], zrecv.at[0], (zdn, gy)),
        remote(zsrc.at[1], got.at[0], zsend.at[1], zrecv.at[1], (zup, gy)),
    ]
    c_copies = [
        remote(corner.at[0], got_corner.at[1, 1], csend.at[0], crecv.at[0], (zdn, ydn)),
        remote(corner.at[0], got_corner.at[1, 0], csend.at[1], crecv.at[1], (zdn, yup)),
        remote(corner.at[1], got_corner.at[0, 1], csend.at[2], crecv.at[2], (zup, ydn)),
        remote(corner.at[1], got_corner.at[0, 0], csend.at[3], crecv.at[3], (zup, yup)),
    ]
    y_copies = [
        remote(s0.at[:, :, pl.ds(2, 2)], s0.at[:, :, pl.ds(NY + 2, 2)], ysend.at[0], yrecv.at[0], (gz, ydn)),
        remote(s0.at[:, :, pl.ds(NY, 2)], s0.at[:, :, pl.ds(0, 2)], ysend.at[1], yrecv.at[1], (gz, yup)),
        remote(mk.at[:, 1], mk.at[:, NY + 1], ysend.at[2], yrecv.at[2], (gz, ydn)),
        remote(mk.at[:, NY], mk.at[:, 0], ysend.at[3], yrecv.at[3], (gz, yup)),
    ]
    for cp in z_copies + c_copies + y_copies:
        cp.start()
    bottom, top = gz == 0, gz == NGZ - 1

    def rows(src, j, below, above):
        halves = []
        ca = [src[f, 0, j] for f in range(4)]
        cb = [src[f, 1, j] for f in range(4)]
        ap = [pltpu.roll(v, 1, 1) for v in ca]
        bp = [pltpu.roll(v, 1, 1) for v in cb]
        am = [pltpu.roll(v, LANES - 1, 1) for v in ca]
        bm = [pltpu.roll(v, LANES - 1, 1) for v in cb]
        for h, c in ((0, ca), (1, cb)):
            if h == 0:
                lo = ap if below is None else [jnp.where(first, below[f], ap[f]) for f in range(4)]
                up = [jnp.where(last, bm[f], am[f]) for f in range(4)]
            else:
                lo = [jnp.where(first, ap[f], bp[f]) for f in range(4)]
                up = bm if above is None else [jnp.where(last, above[f], bm[f]) for f in range(4)]
            ew = [around_x(v) for v in c]
            n = [src[f, h, j + 1] for f in range(4)]
            s = [src[f, h, j - 1] for f in range(4)]
            halves.append(advance(c, [p[0] for p in ew], [p[1] for p in ew], n, s, up, lo))
        return ca, cb, halves

    def row_one(y, ends):
        below, above = ends
        halves = rows(s0, y + 2, below, above)[2]
        for h in range(2):
            m = mk[h, y + 1].astype(F32)
            s1[0, h, y + 1] = halves[h][0]
            for f in range(1, 4):
                s1[f, h, y + 1] = halves[h][f] * m

    def loop_one(y, carry):
        row_one(y, (None, None))
        return carry

    lax.fori_loop(1, NY - 1, loop_one, 0, unroll=UNROLL)

    for cp in z_copies + c_copies + y_copies:
        cp.wait()
    loop_one(0, 0)
    loop_one(NY - 1, 0)

    ends = []
    for side in range(2):
        for f in range(4):
            lo = pltpu.roll(got_corner[side, 0], (3 - f) % LANES, 1)
            hi = pltpu.roll(got_corner[side, 1], (LANES - f) % LANES, 1)
            v = jnp.where(last, lo, hi)
            ends.append(jnp.where(bottom if side == 0 else top, 0.0, v))
    end_of = lambda side, f: ends[side * 4 + f]

    row_one(-1, (
        [pltpu.roll(end_of(0, f), 1, 1) for f in range(4)],
        [end_of(1, f) for f in range(4)],
    ))
    row_one(NY, (
        [end_of(0, f) for f in range(4)],
        [pltpu.roll(end_of(1, f), LANES - 1, 1) for f in range(4)],
    ))
    for side in range(2):
        for f in range(5):
            for k in range(4):
                g = got[side, f, k // 2]
                if side == 0 and k % 2 == 1:
                    g = pltpu.roll(g, LANES - 2, 1)
                if side == 1 and k % 2 == 0:
                    g = pltpu.roll(g, 2, 1)
                if f < 4:
                    g = jnp.where(bottom if side == 0 else top, 0.0, g)
                near = own[f, k]
                merged[side, f, k + 1] = jnp.where(low2, g, near) if side == 0 else jnp.where(low2, near, g)
        for f in range(4):
            end = end_of(side, f)
            before = jnp.where(lane == 1 + side, pltpu.roll(end, 2 + side, 1), pltpu.roll(s0[f, side, 1], 2, 1))
            after = jnp.where(
                lane == 125 + side, pltpu.roll(end, 125 + side, 1), pltpu.roll(s0[f, side, NY + 2], 126, 1)
            )
            merged[side, f, 0] = jnp.where(lane < 4, before, pltpu.roll(merged[side, f, 4], 4, 1))
            merged[side, f, 5] = jnp.where(lane >= 124, after, pltpu.roll(merged[side, f, 1], 124, 1))

        def edge(k, carry, side=side):
            c = [merged[side, f, k + 1] for f in range(4)]
            n = [merged[side, f, k + 2] for f in range(4)]
            s = [merged[side, f, k] for f in range(4)]
            lo = [pltpu.roll(v, 1, 1) for v in c]
            up = [pltpu.roll(v, LANES - 1, 1) for v in c]
            ew = [around_x(v) for v in c]
            new = advance(c, [p[0] for p in ew], [p[1] for p in ew], n, s, up, lo)
            m = merged[side, 4, k + 1]
            for f in range(4):
                edges[side, f, k] = new[f] if f == 0 else new[f] * m
            return carry

        lax.fori_loop(0, 4, edge, 0, unroll=2)

    def unpack(k, carry):
        for f in range(4):
            b, t = edges[0, f, k], edges[1, f, k]
            inner = jnp.where(low2, t, b)
            outer = jnp.where(
                low2,
                jnp.where(top, 0.0, pltpu.roll(t, LANES - 1, 1)),
                jnp.where(bottom, 0.0, pltpu.roll(b, 1, 1)),
            )
            for j in range(32):
                y = 4 * j + k
                shift = (2 * LANES - 4 * j - 2) % LANES
                v = pltpu.roll(inner, shift, 1)
                s1[f, 0, y + 1] = jnp.where(first, v, s1[f, 0, y + 1])
                s1[f, 1, y + 1] = jnp.where(last, v, s1[f, 1, y + 1])
                ring[f, y] = pltpu.roll(outer, shift, 1)
        return carry

    lax.fori_loop(0, 4, unpack, 0)

    def row_sum(y, pair, acc):
        total = (1.0 - jnp.exp(-0.125 * pair[0])) + (1.0 - jnp.exp(-0.125 * pair[1]))
        return jnp.where(lane == y, jnp.sum(total, axis=1, keepdims=True), acc)

    def loop_two(i, carry):
        acc, warm = carry
        y0 = i * ROWS
        new = []
        for r in range(ROWS):
            y = y0 + r
            past = [ring[f, y] for f in range(4)]
            halves = rows(s1, y + 1, past, past)[2]
            pair = []
            for h in range(2):
                m = 0.5 * mk[h, y + 1].astype(F32)
                for f in range(4):
                    v = s0[f, h, y + 2] + halves[h][f]
                    v = 0.5 * v if f == 0 else v * m
                    res[f, h, y] = v
                    if f == 0:
                        pair.append(v)
            new.append(tuple(pair))
        for r in range(ROWS):
            acc = row_sum(y0 + r - ROWS, warm[r], acc)
        return acc, tuple(new)

    res[0, 0, 0] = zero
    blank = res[0, 0, 0]
    acc, warm = lax.fori_loop(0, NY // ROWS, loop_two, (blank, ((blank, blank),) * ROWS))
    for r in range(ROWS):
        acc = row_sum(NY - ROWS + r, warm[r], acc)

    part[...] = acc
    copies = []
    for d in range(1, NGZ):
        peer = lax.rem(gz + d, NGZ)
        copies.append(remote(
            part.at[pl.ds(peer, 1)], got_part.at[d - 1], psend.at[d - 1], precv.at[d - 1], (peer, gy),
        ))
    for cp in copies:
        cp.start()
    total = part[pl.ds(gz, 1)]
    for cp in copies:
        cp.wait()
    for d in range(NGZ - 1):
        total = total + got_part[d]
    path[...] = total * (8.0 / math.sqrt(2048.0))


def emit(res, path, t_out, u_out, v_out, w_out, path_out, out_sem):
    outs = (t_out, u_out, v_out, w_out)
    for f in range(4):
        for h in range(2):
            for x in range(NX):
                pltpu.make_async_copy(
                    res.at[f, h, :, x, :],
                    outs[f].at[x, :, pl.ds(h * LANES, LANES)],
                    out_sem.at[f],
                ).start()
    path_out[...] = path[...]
    for f in range(4):
        whole = res.at[f]
        pltpu.make_async_copy(whole, whole, out_sem.at[f]).wait()


def on_device(*args):
    block = jax.ShapeDtypeStruct((NX, NY, 2 * LANES), F32)
    line = jax.ShapeDtypeStruct((1, NY), F32)
    anywhere = pl.BlockSpec(memory_space=pl.ANY)
    inside = pl.BlockSpec(memory_space=pltpu.VMEM)
    res, path = pl.pallas_call(
        kernel,
        out_shape=(pltpu.VMEM((4, 2, NY, NX, LANES), F32), pltpu.VMEM((1, NY), F32)),
        in_specs=[anywhere] * 5,
        out_specs=(inside, inside),
        scratch_shapes=[
            pltpu.VMEM((4, 2, NY + 4, NX, LANES), F32),
            pltpu.VMEM((4, 2, NY + 2, NX, LANES), F32),
            pltpu.VMEM((2, NY + 2, NX, LANES), jnp.int32),
            pltpu.VMEM((5, 4, NX, LANES), F32),
            pltpu.VMEM((2, 5, 2, NX, LANES), F32),
            pltpu.VMEM((2, 5, 2, NX, LANES), F32),
            pltpu.VMEM((2, 5, 6, NX, LANES), F32),
            pltpu.VMEM((2, 4, 4, NX, LANES), F32),
            pltpu.VMEM((2, NX, LANES), F32),
            pltpu.VMEM((2, 2, NX, LANES), F32),
            pltpu.VMEM((4, NY, NX, LANES), F32),
            pltpu.VMEM((NX, LANES), F32),
            pltpu.VMEM((NGZ - 1, 1, LANES), F32),
            pltpu.SemaphoreType.DMA((5,)),
            pltpu.SemaphoreType.DMA((4,)),
            pltpu.SemaphoreType.DMA((4,)),
            pltpu.SemaphoreType.DMA((2,)),
            pltpu.SemaphoreType.DMA((2,)),
            pltpu.SemaphoreType.DMA((4,)),
            pltpu.SemaphoreType.DMA((4,)),
            pltpu.SemaphoreType.DMA((NGZ - 1,)),
            pltpu.SemaphoreType.DMA((NGZ - 1,)),
        ],
        compiler_params=pltpu.CompilerParams(
            collective_id=0, has_side_effects=True, vmem_limit_bytes=59 * 1024 * 1024
        ),
        name="flow",
    )(*args)
    return pl.pallas_call(
        emit,
        out_shape=(block, block, block, block, line),
        in_specs=[inside, inside],
        out_specs=(anywhere,) * 4 + (inside,),
        scratch_shapes=[pltpu.SemaphoreType.DMA((4,))],
        compiler_params=pltpu.CompilerParams(vmem_limit_bytes=8 * 1024 * 1024),
        name="emit",
    )(res, path)


def solution(mesh):
    split = P(None, "gy", "gz")
    return jax.shard_map(
        on_device,
        mesh=mesh,
        in_specs=(split,) * 5,
        out_specs=(split,) * 4 + (P("gz", "gy"),),
        check_vma=False,
    )
```
